32 devices in a mesh: section: 2 (over core), tensor: 2 (over x), dp: 8 (over z, y).
Axes of the slice: x: 2, y: 2, z: 4, core: 2. Of those that a mesh axis runs over, the one named last changes fastest.
Arguments:
- exit_hidden: bfloat16 [64, 4, 2048], P('dp', None, ('section', 'tensor')), may hold values from -6 to 6
- exit_depth: int32 [64], P('dp'), may hold values from 0 to 1, as said below
- context_len: int32 [64], P('dp'), may hold values from 48 to 384
- attn_gain: float32 [2, 2048], P('section'), may hold values from 0.1 to 1.9
- w_query: bfloat16 [2, 2048, 2048], P('section', None, 'tensor'), may hold values from -0.125 to 0.125
- w_keyval: bfloat16 [2, 2048, 1024], P('section', None, 'tensor'), may hold values from -0.125 to 0.125
- w_out: bfloat16 [2, 2048, 2048], P('section', 'tensor'), may hold values from -0.125 to 0.125
- kv_cache: bfloat16 [2, 64, 384, 8, 128], P('section', 'dp', None, 'tensor'), may hold values from -400 to 400
- mlp_gain: float32 [2, 2048], P('section'), may hold values from 0.1 to 1.9
- w_gate: bfloat16 [2, 2048, 4096], P('section', 'dp', 'tensor'), may hold values from -0.125 to 0.125
- w_up: bfloat16 [2, 2048, 4096], P('section', 'dp', 'tensor'), may hold values from -0.125 to 0.125
- w_down: bfloat16 [2, 2048, 4096], P('section', 'dp', 'tensor'), may hold values from -0.09375 to 0.09375
Outputs:
- layer_states: bfloat16 [2, 64, 4, 2048], P('section', 'dp', None, 'tensor')
The draws below stay inside these ranges and needn't reach their ends.
Inputs may be any that keep to these rules, and one draw needn't show every extreme that they name: `exit_depth`: every depth from 0 to 1 is held by some request.
All inputs are finite; a program needn't handle non-finite values.
Results may differ from the reference program's by a relative error of at most 0.019.
Values may be sent and summed in bfloat16 or wider, within the bound.
A program may use at most 192 MiB of HBM per device.

```python
import math
import jax
import jax.numpy as jnp
from jax import lax

D = 2048
HEADS = 32
KV_HEADS = 8
HD = 64
FF = 4096
DRAFT = 4
CTX = 384
REQUESTS = 64
LAYERS = 2


def draw_exit_depth(key, part):
    first_key, second_key, order_key = jax.random.split(jax.random.fold_in(key, 11), 3)
    first = jax.random.randint(first_key, (REQUESTS,), 0, LAYERS)
    second = jax.random.randint(second_key, (REQUESTS,), 0, LAYERS)
    depth = jnp.minimum(first, second).astype(jnp.int32)
    order = jax.random.permutation(order_key, REQUESTS)
    depth = depth.at[order[:LAYERS]].set(jnp.arange(LAYERS, dtype=jnp.int32))
    return depth.astype(jnp.int32)


def draw_kv_cache(key, part):
    base = jax.random.normal(jax.random.fold_in(key, 21), (LAYERS, REQUESTS, CTX, KV_HEADS, 2 * HD), jnp.float32)
    return base.astype(jnp.bfloat16)


def with_ends(entries, stream_key, least, largest):
    longest = entries.shape.index(max(entries.shape))
    spots = []
    for shift in (0, 1):
        where = [jax.random.randint(jax.random.fold_in(stream_key, axis), (), 0, length) for axis, length in enumerate(entries.shape)]
        where[longest] = (where[longest] + shift) % entries.shape[longest]
        spots.append(tuple(where))
    return entries.at[spots[0]].set(least).at[spots[1]].set(largest)


def steps_of(key, dims, cuts, smallest, high):
    def one(dim, parts):
        heights = jax.random.uniform(jax.random.fold_in(jax.random.fold_in(key, 6), dim), (parts,), jnp.float32, smallest / len(cuts), high / len(cuts))
        return jnp.repeat(jnp.exp(heights), dims[dim] // parts).reshape((-1,) + (1,) * (len(dims) - dim - 1))

    level = one(*cuts[0])
    for cut in cuts[1:]:
        level = level * one(*cut)
    return level


def noise(key, dims, deviation, limit, shards=(), kind=jnp.bfloat16):
    result = deviation * jax.random.normal(key, dims, jnp.float32)
    if shards:
        result = result * steps_of(key, dims, shards, -0.22, 0.18)
    return jnp.clip(result, -limit, limit).astype(kind)


def setup_inputs(seed: int = 0) -> dict:
    streams_of = jax.random.split(jax.random.key(seed), 13)
    exit_hidden = noise(streams_of[0], (REQUESTS, DRAFT, D), 1.0, 6.0, ((0, 8), (2, 4)))
    exit_depth = draw_exit_depth(jax.random.fold_in(streams_of[12], 71), 0)
    context_len = with_ends(jax.random.randint(streams_of[2], (REQUESTS,), CTX // 8, CTX + 1), jax.random.fold_in(streams_of[2], 1), CTX // 8, CTX).astype(jnp.int32)
    attn_gain = jnp.clip(1.0 + 0.18 * jax.random.normal(streams_of[3], (LAYERS, D), jnp.float32), 0.1, 1.9)
    w_query = noise(streams_of[4], (LAYERS, D, HEADS * HD), D ** -0.5, 0.125, ((0, 2), (2, 2)))
    w_keyval = noise(streams_of[5], (LAYERS, D, KV_HEADS * 2 * HD), D ** -0.5, 0.125, ((0, 2), (2, 2)))
    w_out = noise(streams_of[6], (LAYERS, HEADS * HD, D), (HEADS * HD) ** -0.5, 0.125, ((0, 2), (1, 2)))
    kv_cache = draw_kv_cache(jax.random.fold_in(streams_of[12], 71), 0)
    mlp_gain = jnp.clip(1.0 + 0.18 * jax.random.normal(streams_of[8], (LAYERS, D), jnp.float32), 0.1, 1.9)
    w_gate = noise(streams_of[9], (LAYERS, D, FF), D ** -0.5, 0.125, ((0, 2), (1, 8), (2, 2)))
    w_up = noise(streams_of[10], (LAYERS, D, FF), D ** -0.5, 0.125, ((0, 2), (1, 8), (2, 2)))
    w_down = noise(streams_of[11], (LAYERS, D, FF), FF ** -0.5, 0.09375, ((0, 2), (1, 8), (2, 2)))
    return {"exit_hidden": exit_hidden, "exit_depth": exit_depth, "context_len": context_len, "attn_gain": attn_gain, "w_query": w_query, "w_keyval": w_keyval, "w_out": w_out, "kv_cache": kv_cache, "mlp_gain": mlp_gain, "w_gate": w_gate, "w_up": w_up, "w_down": w_down}


EPS = 1e-05
THETA = 500000.0
NEGATIVE = -1e+30

def rotate(values, where_at):
    middle = values.shape[-1] // 2
    rates = jnp.exp(jnp.arange(middle, dtype=jnp.float32) * (-2.0 * math.log(THETA) / values.shape[-1]))
    angles = where_at.astype(jnp.float32)[..., None] * rates
    cosine = jnp.cos(angles)
    sine = jnp.sin(angles)
    first = values[..., :middle]
    second = values[..., middle:]
    return jnp.concatenate([first * cosine - second * sine, second * cosine + first * sine], axis=-1)

def normalize(hidden, gain):
    wide = hidden.astype(jnp.float32)
    factor = lax.rsqrt(lax.optimization_barrier(jnp.mean(wide * wide, axis=-1, keepdims=True)) + EPS)
    return (wide * factor * gain).astype(jnp.bfloat16)

def attend(normed, lengths, cache, w_query, w_keyval, w_out):
    rows, drafts, width = normed.shape
    head_size = cache.shape[-1] // 2
    kv_count = cache.shape[2]
    q_count = w_query.shape[-1] // head_size
    group = q_count // kv_count
    flat = normed.reshape(rows * drafts, width)
    query = jnp.dot(flat, w_query, preferred_element_type=jnp.float32).reshape(rows, drafts, kv_count, group, head_size)
    keyval = jnp.dot(flat, w_keyval, preferred_element_type=jnp.float32).reshape(rows, drafts, kv_count, 2 * head_size)
    places = lengths[:, None] + jnp.arange(drafts, dtype=jnp.int32)[None, :]
    query = rotate(query, places[:, :, None, None]).astype(jnp.bfloat16)
    fresh_keys = rotate(keyval[..., :head_size], places[:, :, None]).astype(jnp.bfloat16)
    fresh_values = keyval[..., head_size:].astype(jnp.bfloat16)
    cached_keys = cache[..., :head_size].astype(jnp.float32)
    cached_values = cache[..., head_size:].astype(jnp.float32)
    scale = head_size ** (-0.5)
    query_wide = query.astype(jnp.float32)
    old_scores = jnp.einsum('rjkgd,rpkd->rkgjp', query_wide, cached_keys, precision=lax.Precision.HIGHEST) * scale
    live = jnp.arange(cache.shape[1], dtype=jnp.int32)[None, :] < lengths[:, None]
    old_scores = jnp.where(live[:, None, None, None, :], old_scores, NEGATIVE)
    new_scores = jnp.einsum('rjkgd,rikd->rkgji', query_wide, fresh_keys.astype(jnp.float32), precision=lax.Precision.HIGHEST) * scale
    causal = jnp.arange(drafts)[None, :] <= jnp.arange(drafts)[:, None]
    new_scores = jnp.where(causal, new_scores, NEGATIVE)
    top = jnp.maximum(old_scores.max(axis=-1), new_scores.max(axis=-1))[..., None]
    old_weights = jnp.exp(old_scores - top)
    new_weights = jnp.exp(new_scores - top)
    total = old_weights.sum(axis=-1, keepdims=True) + new_weights.sum(axis=-1, keepdims=True)
    old_weights = (old_weights / total).astype(jnp.bfloat16).astype(jnp.float32)
    new_weights = (new_weights / total).astype(jnp.bfloat16).astype(jnp.float32)
    mixed = jnp.einsum('rkgjp,rpkd->rjkgd', old_weights, cached_values, precision=lax.Precision.HIGHEST)
    mixed = mixed + jnp.einsum('rkgji,rikd->rjkgd', new_weights, fresh_values.astype(jnp.float32), precision=lax.Precision.HIGHEST)
    heads_out = mixed.astype(jnp.bfloat16).reshape(rows * drafts, q_count * head_size)
    return jnp.dot(heads_out, w_out, preferred_element_type=jnp.float32)

def feed_forward(normed, w_gate, w_up, w_down):
    flat = normed.reshape(-1, normed.shape[-1])
    gate = jnp.dot(flat, w_gate, preferred_element_type=jnp.float32)
    up = jnp.dot(flat, w_up, preferred_element_type=jnp.float32)
    act = (jax.nn.silu(gate) * up).astype(jnp.bfloat16)
    return jnp.dot(act, w_down.T, preferred_element_type=jnp.float32)

def reference(exit_hidden, exit_depth, context_len, attn_gain, w_query, w_keyval, w_out, kv_cache, mlp_gain, w_gate, w_up, w_down):
    current = exit_hidden
    states = []
    for layer in range(LAYERS):
        take = (exit_depth >= layer)[:, None, None]
        keep = (exit_depth <= layer)[:, None, None]
        whole = jnp.where(take, exit_hidden, current)
        partial_value = attend(normalize(whole, attn_gain[layer]), context_len, kv_cache[layer], w_query[layer], w_keyval[layer], w_out[layer])
        middle = (whole.astype(jnp.float32) + partial_value.reshape(whole.shape)).astype(jnp.bfloat16)
        branch = feed_forward(normalize(middle, mlp_gain[layer]), w_gate[layer], w_up[layer], w_down[layer])
        updated = (middle.astype(jnp.float32) + branch.reshape(whole.shape)).astype(jnp.bfloat16)
        current = jnp.where(keep, updated, whole)
        states.append(current)
    return jnp.stack(states)
```

```python
import math

import functools

import jax
import jax.numpy as jnp
from jax import lax
from jax.experimental import pallas as pl
from jax.experimental.pallas import tpu as pltpu
from jax.sharding import PartitionSpec as P

D = 2048
DRAFT = 4
CTX = 384
R_DEV = 8


EPS = 1e-05
THETA = 500000.0
NEGATIVE = -1e30


def shifted(array, axis, by):
    length = lax.axis_size(axis)
    pairs = [(i, i + by) for i in range(length) if 0 <= i + by < length]
    return lax.ppermute(array, axis, pairs)


def rotate(values, where_at):
    middle = values.shape[-1] // 2
    rates = jnp.exp(
        jnp.arange(middle, dtype=jnp.float32) * (-2.0 * math.log(THETA) / values.shape[-1])
    )
    angles = where_at.astype(jnp.float32)[..., None] * rates
    cosine = jnp.cos(angles)
    sine = jnp.sin(angles)
    first = values[..., :middle]
    second = values[..., middle:]
    return jnp.concatenate(
        [first * cosine - second * sine, second * cosine + first * sine], axis=-1
    )


def normalize(hidden, gain):
    wide = hidden.astype(jnp.float32)
    factor = lax.rsqrt(jnp.mean(wide * wide, axis=-1, keepdims=True) + EPS)
    return (wide * factor * gain).astype(jnp.bfloat16)


def attend(normed, lengths, cache, w_query, w_keyval, w_out):
    rows, drafts, width = normed.shape
    head_size = cache.shape[-1] // 2
    kv_count = cache.shape[2]
    q_count = w_query.shape[-1] // head_size
    group = q_count // kv_count
    flat = normed.reshape(rows * drafts, width)
    query = jnp.dot(flat, w_query, preferred_element_type=jnp.float32).reshape(
        rows, drafts, kv_count, group, head_size
    )
    keyval = jnp.dot(flat, w_keyval, preferred_element_type=jnp.float32).reshape(
        rows, drafts, kv_count, 2 * head_size
    )
    places = lengths[:, None] + jnp.arange(drafts, dtype=jnp.int32)[None, :]
    query = rotate(query, places[:, :, None, None]).astype(jnp.bfloat16)
    fresh_keys = rotate(keyval[..., :head_size], places[:, :, None]).astype(jnp.bfloat16)
    fresh_values = keyval[..., head_size:].astype(jnp.bfloat16)
    cached_keys = cache[..., :head_size]
    cached_values = cache[..., head_size:]
    scale = head_size ** (-0.5)
    old_scores = (
        jnp.einsum("rjkgd,rpkd->rkgjp", query, cached_keys, preferred_element_type=jnp.float32)
        * scale
    )
    live = jnp.arange(cache.shape[1], dtype=jnp.int32)[None, :] < lengths[:, None]
    old_scores = jnp.where(live[:, None, None, None, :], old_scores, NEGATIVE)
    new_scores = (
        jnp.einsum("rjkgd,rikd->rkgji", query, fresh_keys, preferred_element_type=jnp.float32)
        * scale
    )
    causal = jnp.arange(drafts)[None, :] <= jnp.arange(drafts)[:, None]
    new_scores = jnp.where(causal, new_scores, NEGATIVE)
    top = jnp.maximum(old_scores.max(axis=-1), new_scores.max(axis=-1))[..., None]
    old_weights = jnp.exp(old_scores - top)
    new_weights = jnp.exp(new_scores - top)
    total = old_weights.sum(axis=-1, keepdims=True) + new_weights.sum(axis=-1, keepdims=True)
    old_weights = (old_weights / total).astype(jnp.bfloat16)
    new_weights = (new_weights / total).astype(jnp.bfloat16)
    mixed = jnp.einsum(
        "rkgjp,rpkd->rjkgd", old_weights, cached_values, preferred_element_type=jnp.float32
    )
    mixed = mixed + jnp.einsum(
        "rkgji,rikd->rjkgd", new_weights, fresh_values, preferred_element_type=jnp.float32
    )
    heads_out = mixed.astype(jnp.bfloat16).reshape(rows * drafts, q_count * head_size)
    return jnp.dot(heads_out, w_out, preferred_element_type=jnp.float32)


def feed_forward(normed, gate_full, up_full, down_full):
    flat = normed.reshape(-1, normed.shape[-1])
    gate = jnp.dot(flat, gate_full, preferred_element_type=jnp.float32)
    up = jnp.dot(flat, up_full, preferred_element_type=jnp.float32)
    act = (jax.nn.silu(gate) * up).astype(jnp.bfloat16)
    return lax.dot_general(
        act, down_full, (((1,), (1,)), ((), ())), preferred_element_type=jnp.float32
    )


def local(
    exit_hidden,
    exit_depth,
    context_len,
    attn_gain,
    w_query,
    w_keyval,
    w_out,
    kv_cache,
    mlp_gain,
    w_gate,
    w_up,
    w_down,
):
    entry = lax.all_gather(exit_hidden, ("section", "tensor"), axis=2, tiled=True)
    gate_full, up_full, down_full = (
        lax.all_gather(w_gate[0], "dp", axis=0, tiled=True),
        lax.all_gather(w_up[0], "dp", axis=0, tiled=True),
        lax.all_gather(w_down[0], "dp", axis=0, tiled=True),
    )
    section = lax.axis_index("section")
    sections = lax.axis_size("section")
    pieces = 1
    members = R_DEV // pieces
    share = D // lax.axis_size("tensor")
    offset = lax.axis_index("tensor") * share
    entry = entry.reshape(pieces, members, DRAFT, D)
    depth = exit_depth.reshape(pieces, members)
    length = context_len.reshape(pieces, members)
    cache = kv_cache[0].reshape(pieces, members, CTX, kv_cache.shape[3], kv_cache.shape[4])
    gain = attn_gain[0]
    second_gain = mlp_gain[0]
    query_weight = w_query[0]
    keyval_weight = w_keyval[0]
    out_weight = w_out[0]

    def turn_step(turn, carry):
        received, outputs = carry
        block = turn - section
        valid = (block >= 0) & (block < pieces)
        index = jnp.clip(block, 0, pieces - 1)
        block_depth = depth[index]
        block_length = length[index]
        block_entry = entry[index]
        block_cache = cache[index]
        take = (block_depth >= section)[:, None, None]
        keep = (block_depth <= section)[:, None, None]
        active = valid & jnp.any(block_depth <= section)

        def compute(whole):
            return attend(
                normalize(whole, gain),
                block_length,
                block_cache,
                query_weight,
                keyval_weight,
                out_weight,
            )

        def branch_work(middle):
            return feed_forward(normalize(middle, second_gain), gate_full, up_full, down_full)

        def skipped(whole):
            return jnp.zeros((members * DRAFT, D), jnp.float32)

        whole = jnp.where(take, block_entry, received)
        partial_value = lax.cond(active, compute, skipped, whole)
        summed = lax.psum(partial_value, "tensor").reshape(members, DRAFT, D)
        middle = (whole.astype(jnp.float32) + summed).astype(jnp.bfloat16)
        branch = lax.cond(active, branch_work, skipped, middle)
        branch_sum = (
            lax.psum(branch.astype(jnp.bfloat16), "tensor")
            .astype(jnp.float32)
            .reshape(members, DRAFT, D)
        )
        updated = (middle.astype(jnp.float32) + branch_sum).astype(jnp.bfloat16)
        result = jnp.where(keep, updated, whole)
        own = lax.dynamic_slice_in_dim(result, offset, share, 2)
        stored = jnp.where(valid, own, outputs[index])
        outputs = lax.dynamic_update_index_in_dim(outputs, stored, index, 0)
        received = shifted(result, "section", 1)
        return (received, outputs)

    carried = D
    start = (
        jnp.zeros((members, DRAFT, carried), jnp.bfloat16),
        jnp.zeros((pieces, members, DRAFT, share), jnp.bfloat16),
    )
    final = lax.fori_loop(0, sections + pieces - 1, turn_step, start)
    return final[1]


MESH = pl.DeviceIdType.MESH
BF = jnp.bfloat16
F32 = jnp.float32


def bits(size):
    return size.bit_length() - 1


def mm(a, b):
    return jnp.dot(a, b, preferred_element_type=F32)


def mm_t(a, b):
    return lax.dot_general(a, b, (((1,), (1,)), ((), ())), preferred_element_type=F32)


def lanes_like(shape):
    return lax.broadcasted_iota(jnp.int32, shape, len(shape) - 1)


def fused_kernel(
    ndp,
    lens_ref,
    depth_ref,
    cos_ref,
    sin_ref,
    gain_ref,
    gain2_ref,
    entry_ref,
    wq_hbm,
    wkv_hbm,
    kv_hbm,
    wo_hbm,
    wg_hbm,
    wu_hbm,
    wd_hbm,
    out_ref,
    wq, wkv, kv, wo, wg, wu, wd,
    ent, cur, whb, qs, kvs, qp, ns, oh, heads,
    p1, mids, mid, xs, sqs, sqr,
    ybuf, yrec, acc, zbuf, zrec, acts, fbuf, fin, res,
    ld_sem, ent_s, ent_r, a_s, a_r, q_s, q_r, y_s, y_r, z_s, z_r,
    g_s, g_r, h_s, f_s, f_r, c_s, c_r,
):
    s = lax.axis_index("section")
    t = lax.axis_index("tensor")
    d = lax.axis_index("dp")
    half = ndp // 2
    z = d // 2
    y = d % 2
    tok, width = cos_ref.shape[0], gain_ref.shape[1]
    fb = width // ndp
    reqs = lens_ref.shape[0]
    drafts = tok // reqs
    n_heads = wq.shape[1] // 64
    n_kv = wkv.shape[1] // 128
    ff = wg.shape[1]
    rows = n_heads * drafts

    loads = [
        pltpu.make_async_copy(src, dst, ld_sem.at[i])
        for i, (src, dst) in enumerate(
            [(wq_hbm, wq), (wkv_hbm, wkv), (kv_hbm, kv), (wo_hbm, wo), (wg_hbm, wg), (wu_hbm, wu), (wd_hbm, wd)]
        )
    ]
    for one in loads:
        one.start()

    barrier = pltpu.get_barrier_semaphore()
    for k in range(1, 2 * ndp):
        peer = (t * ndp + d + k) % (2 * ndp)
        pl.semaphore_signal(barrier, inc=1, device_id=(s, peer // ndp, peer % ndp), device_id_type=MESH)
    for k in range(2):
        pl.semaphore_signal(barrier, inc=1, device_id=(1 - s, k, d), device_id_type=MESH)
    pl.semaphore_wait(barrier, 2 * ndp + 1)

    def remote(src, dst, send, recv, where):
        return pltpu.make_async_remote_copy(
            src_ref=src, dst_ref=dst, send_sem=send, recv_sem=recv, device_id=where, device_id_type=MESH
        )

    mine = s * 2 + t
    pending = []
    for k in range(1, 4):
        other = (mine + k) % 4
        copy = remote(entry_ref, ent.at[mine], ent_s.at[k - 1], ent_r.at[mine], (other // 2, other % 2, d))
        copy.start()
        pending.append(copy)
    ent[mine] = entry_ref[...]

    def permutation(transposed):
        i = lax.broadcasted_iota(jnp.int32, (n_heads * tok,) * 2, 1 if transposed else 0)
        c = lax.broadcasted_iota(jnp.int32, (n_heads * tok,) * 2, 0 if transposed else 1)
        bd, bt, br = bits(drafts), bits(tok), bits(rows)
        target = ((i & (rows - 1)) >> bd << bt) + (i >> br << bd) + (i & (drafts - 1))
        return jnp.where(target == c, 1.0, 0.0).astype(BF)

    for k in range(1, 4):
        other = (mine + k) % 4
        remote(entry_ref, ent.at[other], ent_s.at[k - 1], ent_r.at[other], (other // 2, other % 2, d)).wait_recv()

    @pl.when(s == 0)
    def _():
        cur[...] = jnp.zeros_like(cur)

    @pl.when(s == 1)
    def _():
        for k in range(2):
            remote(res, cur.at[k], c_s.at[k], c_r.at[k], (0, k, d)).wait_recv()

    depth = depth_ref[...][:, :1]
    take = depth >= s
    keep = depth <= s
    wide = []
    total_sq = None
    per_ent = ent.shape[2] // fb
    per_cur = cur.shape[2] // fb
    for b in range(ndp):
        e = ent[b // per_ent, :, (b % per_ent) * fb : (b % per_ent + 1) * fb].astype(F32)
        c = cur[b // per_cur, :, (b % per_cur) * fb : (b % per_cur + 1) * fb].astype(F32)
        w = jnp.where(take, e, c)
        whb[b] = w.astype(BF)
        wide.append(w)
        sq = jnp.sum(w * w, axis=-1, keepdims=True)
        total_sq = sq if total_sq is None else total_sq + sq
    factor = lax.rsqrt(total_sq * (1.0 / width) + EPS)
    normed = jnp.concatenate(
        [(w * factor * gain_ref[:, b * fb : (b + 1) * fb]).astype(BF) for b, w in enumerate(wide)], axis=1
    )

    loads[0].wait()
    for i in range(wq.shape[1] // 256):
        qs[:, i * 256 : (i + 1) * 256] = mm(normed, wq[:, i * 256 : (i + 1) * 256])
    loads[1].wait()
    for i in range(wkv.shape[1] // 256):
        kvs[:, i * 256 : (i + 1) * 256] = mm(normed, wkv[:, i * 256 : (i + 1) * 256])

    cosine = cos_ref[...]
    sine = sin_ref[...]
    lane = lanes_like((tok, 128))
    low = (lane & 63) < 32
    left = lane < 64

    def turned(x):
        partner = jnp.where(low, pltpu.roll(x, 96, 1), pltpu.roll(x, 32, 1))
        return x * cosine + partner * sine

    stacked = []
    for b in range(n_heads // 2):
        x = turned(qs[:, b * 128 : (b + 1) * 128]) * (64 ** -0.5)
        stacked.append(jnp.where(left, x, 0.0).astype(BF))
        stacked.append(jnp.where(left, pltpu.roll(x, 64, 1), 0.0).astype(BF))
    qp[...] = mm(permutation(False), jnp.concatenate(stacked, axis=0)).astype(BF)
    fresh = []
    for h in range(n_kv):
        x = kvs[:, h * 128 : (h + 1) * 128]
        fresh.append(jnp.where(left, turned(x), x).astype(BF))
    fresh = jnp.concatenate(fresh, axis=0)

    ri = lax.broadcasted_iota(jnp.int32, (reqs * rows, n_kv * tok), 0)
    ci = lax.broadcasted_iota(jnp.int32, (reqs * rows, n_kv * tok), 1)
    bg = bits(rows // n_kv)
    allowed = (
        ((ri >> bits(rows)) == ((ci & (tok - 1)) >> bits(drafts)))
        & (((ri & (rows - 1)) >> bg) == (ci >> bits(tok)))
        & ((ci & (drafts - 1)) <= (ri & (drafts - 1)))
    )
    ns[...] = jnp.where(allowed, mm_t(qp[...], fresh), NEGATIVE)

    loads[2].wait()
    ctx = kv.shape[1] // n_kv
    slot = lax.broadcasted_iota(jnp.int32, (rows, ctx * n_kv), 1)
    group = lax.broadcasted_iota(jnp.int32, (rows, ctx * n_kv), 0) >> bg
    same = (slot & (n_kv - 1)) == group
    for r in range(reqs):
        cached = kv[r]
        old = mm_t(qp[r * rows : (r + 1) * rows], cached)
        old = jnp.where(same & (slot < n_kv * lens_ref[r]), old, NEGATIVE)
        new = ns[r * rows : (r + 1) * rows]
        top = jnp.maximum(jnp.max(old, axis=1, keepdims=True), jnp.max(new, axis=1, keepdims=True))
        old = jnp.exp(old - top)
        new = jnp.exp(new - top)
        total = jnp.sum(old, axis=1, keepdims=True) + jnp.sum(new, axis=1, keepdims=True)
        mixed = mm(old.astype(BF), cached) + mm(new.astype(BF), fresh)
        oh[r * rows : (r + 1) * rows] = (mixed / total).astype(BF)

    back = mm(permutation(True), oh[...])
    for b in range(n_heads // 2):
        first = back[2 * b * tok : (2 * b + 1) * tok]
        second = back[(2 * b + 1) * tok : (2 * b + 2) * tok]
        heads[:, b * 128 : (b + 1) * 128] = jnp.where(left, pltpu.roll(first, 64, 1), second).astype(BF)

    loads[3].wait()
    me = t * ndp + d

    def project(i):
        b = (d + 1 + i) % ndp
        part = mm(heads[...], wo[:, pl.ds(pl.multiple_of(b * fb, fb), fb)])
        p1[b] = (part + 0.5 * whb[b].astype(F32)).astype(BF)
        return b

    def to_all(i, k):
        b = project(i)
        for u in range(2):
            remote(p1.at[b], mids.at[t, d], a_s.at[u * ndp + b], a_r.at[me], (s, u, b)).start()
        return k

    lax.fori_loop(0, ndp - 1, to_all, 0)
    project(ndp - 1)
    remote(p1.at[d], mids.at[t, d], a_s.at[(1 - t) * ndp + d], a_r.at[me], (s, 1 - t, d)).start()
    mids[t, d] = p1[d]

    for k in range(1, 2 * ndp):
        peer = (me + k) % (2 * ndp)
        pt, pd = peer // ndp, peer % ndp
        remote(p1.at[pd], mids.at[pt, pd], a_s.at[peer], a_r.at[peer], (s, pt, pd)).wait_recv()

    gain2 = gain2_ref[pl.ds(d, 1), :]
    for b in range(ndp):
        m = (mids[0, b].astype(F32) + mids[1, b].astype(F32)).astype(BF)
        mid[b] = m
        m = m.astype(F32)
        sq = m * m
        row = sq[:, :128]
        for j in range(1, fb // 128):
            row = row + sq[:, j * 128 : (j + 1) * 128]
        sqs[b] = row
        xs[b % 2, b // 2] = (m * gain2).astype(BF)
    for k in range(1, ndp):
        b = (d + k) % ndp
        remote(sqs.at[b], sqr.at[d], q_s.at[b], q_r.at[d], (s, t, b)).start()
    sqr[d] = sqs[d]

    loads[4].wait()
    loads[5].wait()
    twin = d + 1 - 2 * y
    theirs = xs[1 - y].reshape(half * tok, fb)
    for i in range(ff // 512):
        cols = slice(i * 512, (i + 1) * 512)
        ups = slice(ff + i * 512, ff + (i + 1) * 512)
        ybuf[:, :, cols] = mm(theirs, wg[:, cols]).astype(BF).reshape(half, tok, 512)
        ybuf[:, :, ups] = mm(theirs, wu[:, cols]).astype(BF).reshape(half, tok, 512)
    order = [(z + k) % half for k in range(1, half + 1)]
    for zz in order:
        remote(ybuf.at[zz], yrec.at[zz], y_s.at[zz], y_r.at[zz], (s, t, twin)).start()
    own = xs[y].reshape(half * tok, fb)
    for i in range(ff // 512):
        cols = slice(i * 512, (i + 1) * 512)
        ups = slice(ff + i * 512, ff + (i + 1) * 512)
        acc[:, :, cols] = mm(own, wg[:, cols]).reshape(half, tok, 512)
        acc[:, :, ups] = mm(own, wu[:, cols]).reshape(half, tok, 512)
    for zz in order[:-1]:
        remote(ybuf.at[zz], yrec.at[zz], y_s.at[zz], y_r.at[zz], (s, t, twin)).wait_recv()
        zbuf[zz] = (acc[zz] + yrec[zz].astype(F32)).astype(BF)
        remote(zbuf.at[zz], zrec.at[z], z_s.at[zz], z_r.at[z], (s, t, zz * 2 + y)).start()
    remote(ybuf.at[z], yrec.at[z], y_s.at[z], y_r.at[z], (s, t, twin)).wait_recv()
    for k in range(1, ndp):
        b = (d + k) % ndp
        remote(sqs.at[b], sqr.at[b], q_s.at[b], q_r.at[b], (s, t, b)).wait_recv()
    sums = sqr[0]
    for b in range(1, ndp):
        sums = sums + sqr[b]
    scale = lax.rsqrt(jnp.sum(sums, axis=1, keepdims=True) * (1.0 / width) + EPS)
    for zz in order[:-1]:
        remote(zbuf.at[zz], zrec.at[zz], z_s.at[zz], z_r.at[zz], (s, t, zz * 2 + y)).wait_recv()
    for i in range(ff // 512):
        pair = []
        for start in (i * 512, ff + i * 512):
            cols = slice(start, start + 512)
            v = acc[z, :, cols] + yrec[z, :, cols].astype(F32)
            for zz in order[:-1]:
                v = v + zrec[zz, :, cols].astype(F32)
            pair.append(v * scale)
        gate, up = pair
        acts[y, z, :, i * 512 : (i + 1) * 512] = (gate / (1.0 + jnp.exp(-gate)) * up).astype(BF)

    for zz in order[:-1]:
        remote(acts.at[y, z], acts.at[y, z], g_s.at[zz], g_r.at[y * half + z], (s, t, zz * 2 + y)).start()
    remote(acts.at[y, z], acts.at[y, z], h_s.at[z], g_r.at[y * half + z], (s, t, twin)).start()
    for zz in order[:-1]:
        remote(acts.at[y, zz], acts.at[y, zz], g_s.at[zz], g_r.at[y * half + zz], (s, t, zz * 2 + y)).wait_recv()
        remote(acts.at[y, zz], acts.at[y, zz], h_s.at[zz], g_r.at[y * half + zz], (s, t, twin)).start()

    loads[6].wait()
    home = d // half
    place = t * half + d % half

    def finish(parity):
        hidden = acts[parity].reshape(half * tok, ff)
        grown = mm_t(hidden, wd[...])
        for zz in range(half):
            b = zz * 2 + parity
            value = grown[zz * tok : (zz + 1) * tok] + 0.5 * mid[b].astype(F32)
            fbuf[b] = value.astype(BF)
        for zz in order:
            b = zz * 2 + parity
            away = (b != d) | (home != t)

            @pl.when(away)
            def _():
                remote(fbuf.at[b], fin.at[place], f_s.at[b], f_r.at[place], (s, home, b)).start()

            @pl.when(jnp.logical_not(away))
            def _():
                fin[place] = fbuf[b]

    finish(y)
    for zz in order:
        remote(acts.at[1 - y, zz], acts.at[1 - y, zz], h_s.at[zz], g_r.at[(1 - y) * half + zz], (s, t, twin)).wait_recv()
    finish(1 - y)

    for k in range(ndp):
        src_t, src_d = k // half, t * half + k % half
        own_block = (src_t == t) & (src_d == d)

        @pl.when(jnp.logical_not(own_block))
        def _():
            remote(fbuf.at[0], fin.at[k], f_s.at[0], f_r.at[k], (s, src_t, src_d)).wait_recv()

    for j in range(half):
        updated = (fin[j].astype(F32) + fin[half + j].astype(F32)).astype(BF).astype(F32)
        value = jnp.where(keep, updated, whb[t * half + j].astype(F32)).astype(BF)
        out_ref[:, j * fb : (j + 1) * fb] = value
        res[:, j * fb : (j + 1) * fb] = value

    @pl.when(s == 0)
    def _():
        for k in range(2):
            remote(res, cur.at[t], c_s.at[k], c_r.at[t], (1, k, d)).start()
        for k in range(2):
            remote(res, cur.at[t], c_s.at[k], c_r.at[t], (1, k, d)).wait_send()

    for copy in pending:
        copy.wait_send()
    for k in range(1, 2 * ndp):
        peer = (me + k) % (2 * ndp)
        pt, pd = peer // ndp, peer % ndp
        remote(p1.at[pd], mids.at[t, d], a_s.at[peer], a_r.at[peer], (s, pt, pd)).wait_send()
    for k in range(1, ndp):
        b = (d + k) % ndp
        remote(sqs.at[b], sqr.at[d], q_s.at[b], q_r.at[d], (s, t, b)).wait_send()
    for zz in order:
        remote(ybuf.at[zz], yrec.at[zz], y_s.at[zz], y_r.at[zz], (s, t, twin)).wait_send()
        remote(acts.at[y, zz], acts.at[y, zz], h_s.at[zz], g_r.at[y * half + zz], (s, t, twin)).wait_send()
    for zz in order[:-1]:
        remote(zbuf.at[zz], zrec.at[z], z_s.at[zz], z_r.at[z], (s, t, zz * 2 + y)).wait_send()
        remote(acts.at[y, z], acts.at[y, z], g_s.at[zz], g_r.at[y * half + z], (s, t, zz * 2 + y)).wait_send()
    for b in range(ndp):

        @pl.when((b != d) | (home != t))
        def _():
            remote(fbuf.at[b], fin.at[place], f_s.at[b], f_r.at[place], (s, home, b)).wait_send()


def fused(
    exit_hidden,
    exit_depth,
    context_len,
    attn_gain,
    w_query,
    w_keyval,
    w_out,
    kv_cache,
    mlp_gain,
    w_gate,
    w_up,
    w_down,
):
    ndp = lax.axis_size("dp")
    reqs, drafts, piece = exit_hidden.shape
    tok = reqs * drafts
    width = w_query.shape[1]
    fb = width // ndp
    half = ndp // 2
    ff = w_gate.shape[2]
    n_kv = kv_cache.shape[3]
    ctx = kv_cache.shape[2]
    q_cols = w_query.shape[2]
    n_heads = q_cols // 64
    places = jnp.repeat(context_len, drafts) + jnp.tile(jnp.arange(drafts, dtype=jnp.int32), reqs)
    lane = jnp.arange(128, dtype=jnp.int32)
    rates = jnp.exp((lane % 32).astype(F32) * (-2.0 * math.log(THETA) / 64))
    angles = places.astype(F32)[:, None] * rates
    cosine = jnp.cos(angles)
    sine = jnp.where((lane & 63) < 32, -1.0, 1.0) * jnp.sin(angles)
    depth = jnp.broadcast_to(jnp.repeat(exit_depth, drafts)[:, None], (tok, 128))
    hbm = pl.BlockSpec(memory_space=pl.ANY)
    vmem = pl.BlockSpec(memory_space=pltpu.VMEM)
    smem = pl.BlockSpec(memory_space=pltpu.SMEM)
    dma = pltpu.SemaphoreType.DMA
    V = pltpu.VMEM
    out = pl.pallas_call(
        functools.partial(fused_kernel, ndp),
        out_shape=jax.ShapeDtypeStruct((tok, width // 2), BF),
        in_specs=[smem, vmem, vmem, vmem, vmem, vmem, vmem] + [hbm] * 7,
        out_specs=vmem,
        scratch_shapes=[
            V(w_query.shape[1:], BF),
            V(w_keyval.shape[1:], BF),
            V((reqs, ctx * n_kv, 128), BF),
            V(w_out.shape[1:], BF),
            V(w_gate.shape[1:], BF),
            V(w_up.shape[1:], BF),
            V(w_down.shape[1:], BF),
            V((4, tok, piece), BF),
            V((2, tok, width // 2), BF),
            V((ndp, tok, fb), BF),
            V((tok, q_cols), F32),
            V((tok, n_kv * 128), F32),
            V((n_heads * tok, 128), BF),
            V((n_heads * tok, n_kv * tok), F32),
            V((n_heads * tok, 128), BF),
            V((tok, q_cols), BF),
            V((ndp, tok, fb), BF),
            V((2, ndp, tok, fb), BF),
            V((ndp, tok, fb), BF),
            V((2, half, tok, fb), BF),
            V((ndp, tok, 128), F32),
            V((ndp, tok, 128), F32),
            V((half, tok, 2 * ff), BF),
            V((half, tok, 2 * ff), BF),
            V((half, tok, 2 * ff), F32),
            V((half, tok, 2 * ff), BF),
            V((half, tok, 2 * ff), BF),
            V((2, half, tok, ff), BF),
            V((ndp, tok, fb), BF),
            V((ndp, tok, fb), BF),
            V((tok, width // 2), BF),
            dma((7,)),
            dma((3,)), dma((4,)),
            dma((2 * ndp,)), dma((2 * ndp,)),
            dma((ndp,)), dma((ndp,)),
            dma((half,)), dma((half,)),
            dma((half,)), dma((half,)),
            dma((half,)), dma((ndp,)), dma((half,)),
            dma((ndp,)), dma((ndp,)),
            dma((2,)), dma((2,)),
        ],
        compiler_params=pltpu.CompilerParams(
            collective_id=0, has_side_effects=True, vmem_limit_bytes=60 * 1024 * 1024
        ),
    )(
        context_len,
        depth,
        cosine,
        sine,
        attn_gain,
        mlp_gain.reshape(ndp, fb),
        exit_hidden.reshape(tok, piece),
        w_query[0],
        w_keyval[0],
        kv_cache.reshape(reqs, ctx * n_kv, 128),
        w_out[0],
        w_gate[0],
        w_up[0],
        w_down[0],
    )
    return out.reshape(1, reqs, drafts, width // 2)


def solution(mesh):
    in_specs = (
        P("dp", None, ("section", "tensor")),
        P("dp"),
        P("dp"),
        P("section", None),
        P("section", None, "tensor"),
        P("section", None, "tensor"),
        P("section", "tensor", None),
        P("section", "dp", None, "tensor", None),
        P("section", None),
        P("section", "dp", "tensor"),
        P("section", "dp", "tensor"),
        P("section", "dp", "tensor"),
    )
    out_specs = P("section", "dp", None, "tensor")
    count = mesh.shape["dp"]
    fits = (
        mesh.shape["section"] == 2
        and mesh.shape["tensor"] == 2
        and count & (count - 1) == 0
        and count >= 4
        and (D // count) % 128 == 0
    )
    body = fused if fits else local
    return jax.shard_map(body, mesh=mesh, in_specs=in_specs, out_specs=out_specs, check_vma=False)
```

```python
import math

import functools

import jax
import jax.numpy as jnp
from jax import lax
from jax.experimental import pallas as pl
from jax.experimental.pallas import tpu as pltpu
from jax.sharding import PartitionSpec as P

D = 2048
DRAFT = 4
CTX = 384
R_DEV = 8


EPS = 1e-05
THETA = 500000.0
NEGATIVE = -1e30


def shifted(array, axis, by):
    length = lax.axis_size(axis)
    pairs = [(i, i + by) for i in range(length) if 0 <= i + by < length]
    return lax.ppermute(array, axis, pairs)


def rotate(values, where_at):
    middle = values.shape[-1] // 2
    rates = jnp.exp(
        jnp.arange(middle, dtype=jnp.float32) * (-2.0 * math.log(THETA) / values.shape[-1])
    )
    angles = where_at.astype(jnp.float32)[..., None] * rates
    cosine = jnp.cos(angles)
    sine = jnp.sin(angles)
    first = values[..., :middle]
    second = values[..., middle:]
    return jnp.concatenate(
        [first * cosine - second * sine, second * cosine + first * sine], axis=-1
    )


def normalize(hidden, gain):
    wide = hidden.astype(jnp.float32)
    factor = lax.rsqrt(jnp.mean(wide * wide, axis=-1, keepdims=True) + EPS)
    return (wide * factor * gain).astype(jnp.bfloat16)


def attend(normed, lengths, cache, w_query, w_keyval, w_out):
    rows, drafts, width = normed.shape
    head_size = cache.shape[-1] // 2
    kv_count = cache.shape[2]
    q_count = w_query.shape[-1] // head_size
    group = q_count // kv_count
    flat = normed.reshape(rows * drafts, width)
    query = jnp.dot(flat, w_query, preferred_element_type=jnp.float32).reshape(
        rows, drafts, kv_count, group, head_size
    )
    keyval = jnp.dot(flat, w_keyval, preferred_element_type=jnp.float32).reshape(
        rows, drafts, kv_count, 2 * head_size
    )
    places = lengths[:, None] + jnp.arange(drafts, dtype=jnp.int32)[None, :]
    query = rotate(query, places[:, :, None, None]).astype(jnp.bfloat16)
    fresh_keys = rotate(keyval[..., :head_size], places[:, :, None]).astype(jnp.bfloat16)
    fresh_values = keyval[..., head_size:].astype(jnp.bfloat16)
    cached_keys = cache[..., :head_size]
    cached_values = cache[..., head_size:]
    scale = head_size ** (-0.5)
    old_scores = (
        jnp.einsum("rjkgd,rpkd->rkgjp", query, cached_keys, preferred_element_type=jnp.float32)
        * scale
    )
    live = jnp.arange(cache.shape[1], dtype=jnp.int32)[None, :] < lengths[:, None]
    old_scores = jnp.where(live[:, None, None, None, :], old_scores, NEGATIVE)
    new_scores = (
        jnp.einsum("rjkgd,rikd->rkgji", query, fresh_keys, preferred_element_type=jnp.float32)
        * scale
    )
    causal = jnp.arange(drafts)[None, :] <= jnp.arange(drafts)[:, None]
    new_scores = jnp.where(causal, new_scores, NEGATIVE)
    top = jnp.maximum(old_scores.max(axis=-1), new_scores.max(axis=-1))[..., None]
    old_weights = jnp.exp(old_scores - top)
    new_weights = jnp.exp(new_scores - top)
    total = old_weights.sum(axis=-1, keepdims=True) + new_weights.sum(axis=-1, keepdims=True)
    old_weights = (old_weights / total).astype(jnp.bfloat16)
    new_weights = (new_weights / total).astype(jnp.bfloat16)
    mixed = jnp.einsum(
        "rkgjp,rpkd->rjkgd", old_weights, cached_values, preferred_element_type=jnp.float32
    )
    mixed = mixed + jnp.einsum(
        "rkgji,rikd->rjkgd", new_weights, fresh_values, preferred_element_type=jnp.float32
    )
    heads_out = mixed.astype(jnp.bfloat16).reshape(rows * drafts, q_count * head_size)
    return jnp.dot(heads_out, w_out, preferred_element_type=jnp.float32)


def feed_forward(normed, gate_full, up_full, down_full):
    flat = normed.reshape(-1, normed.shape[-1])
    gate = jnp.dot(flat, gate_full, preferred_element_type=jnp.float32)
    up = jnp.dot(flat, up_full, preferred_element_type=jnp.float32)
    act = (jax.nn.silu(gate) * up).astype(jnp.bfloat16)
    return lax.dot_general(
        act, down_full, (((1,), (1,)), ((), ())), preferred_element_type=jnp.float32
    )


def local(
    exit_hidden,
    exit_depth,
    context_len,
    attn_gain,
    w_query,
    w_keyval,
    w_out,
    kv_cache,
    mlp_gain,
    w_gate,
    w_up,
    w_down,
):
    entry = lax.all_gather(exit_hidden, ("section", "tensor"), axis=2, tiled=True)
    gate_full, up_full, down_full = (
        lax.all_gather(w_gate[0], "dp", axis=0, tiled=True),
        lax.all_gather(w_up[0], "dp", axis=0, tiled=True),
        lax.all_gather(w_down[0], "dp", axis=0, tiled=True),
    )
    section = lax.axis_index("section")
    sections = lax.axis_size("section")
    pieces = 1
    members = R_DEV // pieces
    share = D // lax.axis_size("tensor")
    offset = lax.axis_index("tensor") * share
    entry = entry.reshape(pieces, members, DRAFT, D)
    depth = exit_depth.reshape(pieces, members)
    length = context_len.reshape(pieces, members)
    cache = kv_cache[0].reshape(pieces, members, CTX, kv_cache.shape[3], kv_cache.shape[4])
    gain = attn_gain[0]
    second_gain = mlp_gain[0]
    query_weight = w_query[0]
    keyval_weight = w_keyval[0]
    out_weight = w_out[0]

    def turn_step(turn, carry):
        received, outputs = carry
        block = turn - section
        valid = (block >= 0) & (block < pieces)
        index = jnp.clip(block, 0, pieces - 1)
        block_depth = depth[index]
        block_length = length[index]
        block_entry = entry[index]
        block_cache = cache[index]
        take = (block_depth >= section)[:, None, None]
        keep = (block_depth <= section)[:, None, None]
        active = valid & jnp.any(block_depth <= section)

        def compute(whole):
            return attend(
                normalize(whole, gain),
                block_length,
                block_cache,
                query_weight,
                keyval_weight,
                out_weight,
            )

        def branch_work(middle):
            return feed_forward(normalize(middle, second_gain), gate_full, up_full, down_full)

        def skipped(whole):
            return jnp.zeros((members * DRAFT, D), jnp.float32)

        whole = jnp.where(take, block_entry, received)
        partial_value = lax.cond(active, compute, skipped, whole)
        summed = lax.psum(partial_value, "tensor").reshape(members, DRAFT, D)
        middle = (whole.astype(jnp.float32) + summed).astype(jnp.bfloat16)
        branch = lax.cond(active, branch_work, skipped, middle)
        branch_sum = (
            lax.psum(branch.astype(jnp.bfloat16), "tensor")
            .astype(jnp.float32)
            .reshape(members, DRAFT, D)
        )
        updated = (middle.astype(jnp.float32) + branch_sum).astype(jnp.bfloat16)
        result = jnp.where(keep, updated, whole)
        own = lax.dynamic_slice_in_dim(result, offset, share, 2)
        stored = jnp.where(valid, own, outputs[index])
        outputs = lax.dynamic_update_index_in_dim(outputs, stored, index, 0)
        received = shifted(result, "section", 1)
        return (received, outputs)

    carried = D
    start = (
        jnp.zeros((members, DRAFT, carried), jnp.bfloat16),
        jnp.zeros((pieces, members, DRAFT, share), jnp.bfloat16),
    )
    final = lax.fori_loop(0, sections + pieces - 1, turn_step, start)
    return final[1]


MESH = pl.DeviceIdType.MESH
CHUNKS = 2
BF = jnp.bfloat16
F32 = jnp.float32


def bits(size):
    return size.bit_length() - 1


def mm(a, b):
    return jnp.dot(a, b, preferred_element_type=F32)


def mm_t(a, b):
    return lax.dot_general(a, b, (((1,), (1,)), ((), ())), preferred_element_type=F32)


def lanes_like(shape):
    return lax.broadcasted_iota(jnp.int32, shape, len(shape) - 1)


def fused_kernel(
    ndp,
    lens_ref,
    depth_ref,
    gain_ref,
    gain2_ref,
    entry_ref,
    wq_hbm,
    wkv_hbm,
    kv_hbm,
    wo_hbm,
    wg_hbm,
    wu_hbm,
    wd_hbm,
    out_ref,
    wq, wkv, kv, wo, wg, wu, wd,
    ent, ew, cur, perms, whb, qs, kvs, qp, ns, oh, heads,
    p1, mids, mid, xs, sqs, sqr,
    zbuf, zrec, acts, fbuf, fin, res,
    ld_sem, w_s, w_r, go, ent_s, ent_r, a_s, a_r, q_s, q_r, z_s, z_r,
    g_s, g_r, f_s, f_r, c_s, c_r,
):
    s = lax.axis_index("section")
    t = lax.axis_index("tensor")
    d = lax.axis_index("dp")
    half = ndp // 2
    z = d // 2
    y = d % 2
    twin = d + 1 - 2 * y
    reqs, drafts, piece = entry_ref.shape
    tok = reqs * drafts
    width = gain_ref.shape[1]
    fb = width // half
    n_heads = wq.shape[1] // 64
    n_kv = wkv.shape[1] // 128
    ff = wg.shape[2]
    chunks, cw = acts.shape[0], acts.shape[3]
    rows = n_heads * drafts

    loads = [
        pltpu.make_async_copy(src, dst, ld_sem.at[i])
        for i, (src, dst) in enumerate(
            [
                (wq_hbm, wq),
                (wkv_hbm, wkv),
                (kv_hbm, kv),
                (wo_hbm, wo),
                (wg_hbm, wg.at[y]),
                (wu_hbm, wu.at[y]),
                (wd_hbm, wd.at[y]),
            ]
        )
    ]
    for one in loads:
        one.start()

    barrier = pltpu.get_barrier_semaphore()
    lane_me = t * half + z
    for k in range(1, 2 * half):
        peer = (lane_me + k) % (2 * half)
        where = (s, peer // half, peer % half * 2 + y)
        pl.semaphore_signal(barrier, inc=1, device_id=where, device_id_type=MESH)
    for k in range(2):
        pl.semaphore_signal(barrier, inc=1, device_id=(1 - s, k, d), device_id_type=MESH)
    pl.semaphore_signal(barrier, inc=1, device_id=(s, t, twin), device_id_type=MESH)
    pl.semaphore_wait(barrier, 2 * half + 2)

    def remote(src, dst, send, recv, where):
        return pltpu.make_async_remote_copy(
            src_ref=src, dst_ref=dst, send_sem=send, recv_sem=recv, device_id=where, device_id_type=MESH
        )

    def twin_copy(k):
        src, dst = [(wg_hbm, wg), (wu_hbm, wu), (wd_hbm, wd)][k]
        return remote(src, dst.at[y], w_s.at[k], w_r.at[k], (s, t, twin))

    mine = s * 2 + t
    pending = []
    for k in range(1, 4):
        other = (mine + k) % 4
        copy = remote(entry_ref, ent.at[mine], ent_s.at[k - 1], ent_r.at[mine], (other // 2, other % 2, d))
        copy.start()
        pending.append(copy)
    ent[mine] = entry_ref[...]

    @pl.when(s == 0)
    def _():
        for k in range(3):
            twin_copy(k).start()

    def permutation(transposed):
        i = lax.broadcasted_iota(jnp.int32, (n_heads * tok,) * 2, 1 if transposed else 0)
        c = lax.broadcasted_iota(jnp.int32, (n_heads * tok,) * 2, 0 if transposed else 1)
        bd, bt, br = bits(drafts), bits(tok), bits(rows)
        target = ((i & (rows - 1)) >> bd << bt) + (i >> br << bd) + (i & (drafts - 1))
        return jnp.where(target == c, 1.0, 0.0).astype(BF)

    perms[0] = permutation(False)
    perms[1] = permutation(True)
    row = lax.broadcasted_iota(jnp.int32, (tok, 128), 0)
    lane = lanes_like((tok, 128))
    low = (lane & 63) < 32
    left = lane < 64
    length = jnp.zeros((tok, 128), jnp.int32)
    depth = jnp.zeros((tok, 128), jnp.int32)
    for r in range(reqs):
        here = (row >> bits(drafts)) == r
        length = jnp.where(here, lens_ref[r], length)
        depth = jnp.where(here, depth_ref[r], depth)
    rates = jnp.exp((lane & 31).astype(F32) * (-2.0 * math.log(THETA) / 64))
    angles = (length + (row & (drafts - 1))).astype(F32) * rates
    cosine = jnp.cos(angles)
    sine = jnp.where(low, -1.0, 1.0) * jnp.sin(angles)
    take = depth[:, :1] >= s
    keep = depth[:, :1] <= s

    for k in range(1, 4):
        other = (mine + k) % 4
        remote(entry_ref, ent.at[other], ent_s.at[k - 1], ent_r.at[other], (other // 2, other % 2, d)).wait_recv()

    for q in range(4):
        for r in range(reqs):
            ew[r * drafts : (r + 1) * drafts, q * piece : (q + 1) * piece] = ent[q, r].astype(F32)

    @pl.when(s == 0)
    def _():
        cur[...] = jnp.zeros_like(cur)

    @pl.when(s == 1)
    def _():
        pl.semaphore_wait(go, 1)
        for k in range(3):
            twin_copy(k).start()
        for k in range(2):
            remote(res, cur.at[k], c_s.at[k], c_r.at[k], (0, k, d)).wait_recv()

    wide = []
    total_sq = None
    per_cur = cur.shape[2] // fb
    for b in range(half):
        e = ew[:, b * fb : (b + 1) * fb]
        c = cur[b // per_cur, :, (b % per_cur) * fb : (b % per_cur + 1) * fb].astype(F32)
        w = jnp.where(take, e, c)
        whb[b] = w.astype(BF)
        wide.append(w)
        sq = jnp.sum(w * w, axis=-1, keepdims=True)
        total_sq = sq if total_sq is None else total_sq + sq
    factor = lax.rsqrt(total_sq * (1.0 / width) + EPS)
    normed = jnp.concatenate(
        [(w * factor * gain_ref[:, b * fb : (b + 1) * fb]).astype(BF) for b, w in enumerate(wide)], axis=1
    )

    loads[0].wait()
    for i in range(wq.shape[1] // 256):
        qs[:, i * 256 : (i + 1) * 256] = mm(normed, wq[:, i * 256 : (i + 1) * 256])
    loads[1].wait()
    for i in range(wkv.shape[1] // 256):
        kvs[:, i * 256 : (i + 1) * 256] = mm(normed, wkv[:, i * 256 : (i + 1) * 256])

    def turned(x):
        partner = jnp.where(low, pltpu.roll(x, 96, 1), pltpu.roll(x, 32, 1))
        return x * cosine + partner * sine

    stacked = []
    for b in range(n_heads // 2):
        x = turned(qs[:, b * 128 : (b + 1) * 128]) * (64 ** -0.5)
        stacked.append(jnp.where(left, x, 0.0).astype(BF))
        stacked.append(jnp.where(left, pltpu.roll(x, 64, 1), 0.0).astype(BF))
    qp[...] = mm(perms[0], jnp.concatenate(stacked, axis=0)).astype(BF)
    fresh = []
    for h in range(n_kv):
        x = kvs[:, h * 128 : (h + 1) * 128]
        fresh.append(jnp.where(left, turned(x), x).astype(BF))
    fresh = jnp.concatenate(fresh, axis=0)

    ri = lax.broadcasted_iota(jnp.int32, (reqs * rows, n_kv * tok), 0)
    ci = lax.broadcasted_iota(jnp.int32, (reqs * rows, n_kv * tok), 1)
    bg = bits(rows // n_kv)
    allowed = (
        ((ri >> bits(rows)) == ((ci & (tok - 1)) >> bits(drafts)))
        & (((ri & (rows - 1)) >> bg) == (ci >> bits(tok)))
        & ((ci & (drafts - 1)) <= (ri & (drafts - 1)))
    )
    ns[...] = jnp.where(allowed, mm_t(qp[...], fresh), NEGATIVE)

    loads[2].wait()
    ctx = kv.shape[1] // n_kv
    slot = lax.broadcasted_iota(jnp.int32, (rows, ctx * n_kv), 1)
    group = lax.broadcasted_iota(jnp.int32, (rows, ctx * n_kv), 0) >> bg
    same = (slot & (n_kv - 1)) == group
    for r in range(reqs):
        cached = kv[r]
        old = mm_t(qp[r * rows : (r + 1) * rows], cached)
        old = jnp.where(same & (slot < n_kv * lens_ref[r]), old, NEGATIVE)
        new = ns[r * rows : (r + 1) * rows]
        top = jnp.maximum(jnp.max(old, axis=1, keepdims=True), jnp.max(new, axis=1, keepdims=True))
        old = jnp.exp(old - top)
        new = jnp.exp(new - top)
        total = jnp.sum(old, axis=1, keepdims=True) + jnp.sum(new, axis=1, keepdims=True)
        mixed = mm(old.astype(BF), cached) + mm(new.astype(BF), fresh)
        oh[r * rows : (r + 1) * rows] = (mixed / total).astype(BF)

    back = mm(perms[1], oh[...])
    for b in range(n_heads // 2):
        first = back[2 * b * tok : (2 * b + 1) * tok]
        second = back[(2 * b + 1) * tok : (2 * b + 2) * tok]
        heads[:, b * 128 : (b + 1) * 128] = jnp.where(left, pltpu.roll(first, 64, 1), second).astype(BF)

    loads[3].wait()

    def project(i):
        b = (z + 1 + i) % half
        part = mm(heads[...], wo[:, pl.ds(pl.multiple_of(b * fb, fb), fb)])
        p1[b] = (part + 0.5 * whb[b].astype(F32)).astype(BF)
        return b

    def to_all(i, k):
        b = project(i)
        for u in range(2):
            remote(p1.at[b], mids.at[t, z], a_s.at[u, b], a_r.at[t, z], (s, u, b * 2 + y)).start()
        return k

    lax.fori_loop(0, half - 1, to_all, 0)
    project(half - 1)
    remote(p1.at[z], mids.at[t, z], a_s.at[1 - t, z], a_r.at[t, z], (s, 1 - t, d)).start()
    mids[t, z] = p1[z]

    others = []
    for k in range(1, 2 * half):
        peer = (lane_me + k) % (2 * half)
        others.append((peer // half, peer % half))
    for pt, pz in others:
        remote(p1.at[pz], mids.at[pt, pz], a_s.at[pt, pz], a_r.at[pt, pz], (s, pt, pz * 2 + y)).wait_recv()

    gain2 = gain2_ref[:, pl.ds(pl.multiple_of(z * fb, fb), fb)]
    for b in range(half):
        m = (mids[0, b].astype(F32) + mids[1, b].astype(F32)).astype(BF)
        mid[b] = m
        m = m.astype(F32)
        sq = m * m
        part = sq[:, :128]
        for j in range(1, fb // 128):
            part = part + sq[:, j * 128 : (j + 1) * 128]
        sqs[b] = part
        xs[b] = (m * gain2).astype(BF)
    order = [(z + k) % half for k in range(1, half)]
    for zz in order:
        remote(sqs.at[zz], sqr.at[z], q_s.at[zz], q_r.at[z], (s, t, zz * 2 + y)).start()
    sqr[z] = sqs[z]

    loads[4].wait()
    loads[5].wait()
    for k in range(2):
        twin_copy(k).wait()

    @pl.when(s == 0)
    def _():
        pl.semaphore_signal(go, inc=1, device_id=(1, t, d), device_id_type=MESH)

    grid = xs[...].reshape(half * tok, fb)
    step = 512
    for c in range(chunks):
        for i in range(cw // step):
            src = slice(c * cw + i * step, c * cw + (i + 1) * step)
            for g, w in enumerate((wg, wu)):
                dst = slice(g * cw + i * step, g * cw + (i + 1) * step)
                zbuf[c, :, :, dst] = mm(grid, w[:, :, src].reshape(fb, step)).astype(BF).reshape(half, tok, step)
        for zz in order:
            remote(zbuf.at[c, zz], zrec.at[c, z], z_s.at[c, zz], z_r.at[c, z], (s, t, zz * 2 + y)).start()

    for zz in order:
        remote(sqs.at[zz], sqr.at[zz], q_s.at[zz], q_r.at[zz], (s, t, zz * 2 + y)).wait_recv()
    sums = sqr[0]
    for b in range(1, half):
        sums = sums + sqr[b]
    scale = lax.rsqrt(jnp.sum(sums, axis=1, keepdims=True) * (1.0 / width) + EPS)
    for c in range(chunks):
        for zz in order:
            remote(zbuf.at[c, zz], zrec.at[c, zz], z_s.at[c, zz], z_r.at[c, zz], (s, t, zz * 2 + y)).wait_recv()
        for i in range(cw // step):
            pair = []
            for start in (i * step, cw + i * step):
                cols = slice(start, start + step)
                v = zbuf[c, z, :, cols].astype(F32)
                for zz in order:
                    v = v + zrec[c, zz, :, cols].astype(F32)
                pair.append(v * scale)
            gate, up = pair
            acts[c, z, :, i * step : (i + 1) * step] = (gate / (1.0 + jnp.exp(-gate)) * up).astype(BF)
        for zz in order:
            remote(acts.at[c, z], acts.at[c, z], g_s.at[c, zz], g_r.at[c, z], (s, t, zz * 2 + y)).start()

    loads[6].wait()
    twin_copy(2).wait()
    grown = None
    for c in range(chunks):
        for zz in order:
            remote(acts.at[c, zz], acts.at[c, zz], g_s.at[c, zz], g_r.at[c, zz], (s, t, zz * 2 + y)).wait_recv()
        part = mm_t(acts[c].reshape(half * tok, cw), wd[:, :, c * cw : (c + 1) * cw].reshape(fb, cw))
        grown = part if grown is None else grown + part

    per_home = half // 2
    home = z // per_home
    place = t * per_home + z % per_home
    for b in range(half):
        fbuf[b] = (grown[b * tok : (b + 1) * tok] + 0.5 * mid[b].astype(F32)).astype(BF)
    for zz in order:
        remote(fbuf.at[zz], fin.at[place], f_s.at[zz], f_r.at[place], (s, home, zz * 2 + y)).start()

    @pl.when(home != t)
    def _():
        remote(fbuf.at[z], fin.at[place], f_s.at[z], f_r.at[place], (s, home, d)).start()

    @pl.when(home == t)
    def _():
        fin[place] = fbuf[z]

    for k in range(half):
        src_t, src_z = k // per_home, t * per_home + k % per_home

        @pl.when(jnp.logical_not((src_t == t) & (src_z == z)))
        def _():
            remote(fbuf.at[0], fin.at[k], f_s.at[0], f_r.at[k], (s, src_t, src_z * 2 + y)).wait_recv()

    for j in range(per_home):
        updated = (fin[j].astype(F32) + fin[per_home + j].astype(F32)).astype(BF).astype(F32)
        value = jnp.where(keep, updated, whb[t * per_home + j].astype(F32))
        res[:, j * fb : (j + 1) * fb] = value.astype(BF)
        ew[:, j * fb : (j + 1) * fb] = value

    @pl.when(s == 0)
    def _():
        for k in range(2):
            remote(res, cur.at[t], c_s.at[k], c_r.at[t], (1, k, d)).start()

    for r in range(reqs):
        out_ref[r] = ew[r * drafts : (r + 1) * drafts, : width // 2].astype(BF)

    @pl.when(s == 0)
    def _():
        for k in range(2):
            remote(res, cur.at[t], c_s.at[k], c_r.at[t], (1, k, d)).wait_send()

    for copy in pending:
        copy.wait_send()
    for pt, pz in others:
        remote(p1.at[pz], mids.at[t, z], a_s.at[pt, pz], a_r.at[pt, pz], (s, pt, pz * 2 + y)).wait_send()
    for zz in order:
        remote(sqs.at[zz], sqr.at[z], q_s.at[zz], q_r.at[z], (s, t, zz * 2 + y)).wait_send()
        for c in range(chunks):
            remote(zbuf.at[c, zz], zrec.at[c, z], z_s.at[c, zz], z_r.at[c, z], (s, t, zz * 2 + y)).wait_send()
            remote(acts.at[c, z], acts.at[c, z], g_s.at[c, zz], g_r.at[c, z], (s, t, zz * 2 + y)).wait_send()
        remote(fbuf.at[zz], fin.at[place], f_s.at[zz], f_r.at[place], (s, home, zz * 2 + y)).wait_send()

    @pl.when(home != t)
    def _():
        remote(fbuf.at[z], fin.at[place], f_s.at[z], f_r.at[place], (s, home, d)).wait_send()


def fused(
    exit_hidden,
    exit_depth,
    context_len,
    attn_gain,
    w_query,
    w_keyval,
    w_out,
    kv_cache,
    mlp_gain,
    w_gate,
    w_up,
    w_down,
):
    ndp = lax.axis_size("dp")
    reqs, drafts, piece = exit_hidden.shape
    tok = reqs * drafts
    width = w_query.shape[1]
    half = ndp // 2
    fb = width // half
    ff = w_gate.shape[2]
    n_kv = kv_cache.shape[3]
    ctx = kv_cache.shape[2]
    q_cols = w_query.shape[2]
    n_heads = q_cols // 64
    chunks = CHUNKS
    cw = ff // chunks
    hbm = pl.BlockSpec(memory_space=pl.ANY)
    vmem = pl.BlockSpec(memory_space=pltpu.VMEM)
    smem = pl.BlockSpec(memory_space=pltpu.SMEM)
    dma = pltpu.SemaphoreType.DMA
    V = pltpu.VMEM
    out = pl.pallas_call(
        functools.partial(fused_kernel, ndp),
        out_shape=jax.ShapeDtypeStruct((reqs, drafts, width // 2), BF),
        in_specs=[smem, smem, vmem, vmem, vmem] + [hbm] * 7,
        out_specs=vmem,
        scratch_shapes=[
            V(w_query.shape[1:], BF),
            V(w_keyval.shape[1:], BF),
            V((reqs, ctx * n_kv, 128), BF),
            V(w_out.shape[1:], BF),
            V((2, fb // 2, ff), BF),
            V((2, fb // 2, ff), BF),
            V((2, fb // 2, ff), BF),
            V((4, reqs, drafts, piece), BF),
            V((tok, width), F32),
            V((2, tok, width // 2), BF),
            V((2, n_heads * tok, n_heads * tok), BF),
            V((half, tok, fb), BF),
            V((tok, q_cols), F32),
            V((tok, n_kv * 128), F32),
            V((n_heads * tok, 128), BF),
            V((n_heads * tok, n_kv * tok), F32),
            V((n_heads * tok, 128), BF),
            V((tok, q_cols), BF),
            V((half, tok, fb), BF),
            V((2, half, tok, fb), BF),
            V((half, tok, fb), BF),
            V((half, tok, fb), BF),
            V((half, tok, 128), F32),
            V((half, tok, 128), F32),
            V((chunks, half, tok, 2 * cw), BF),
            V((chunks, half, tok, 2 * cw), BF),
            V((chunks, half, tok, cw), BF),
            V((half, tok, fb), BF),
            V((half, tok, fb), BF),
            V((tok, width // 2), BF),
            dma((7,)),
            dma((3,)), dma((3,)), pltpu.SemaphoreType.REGULAR,
            dma((3,)), dma((4,)),
            dma((2, half)), dma((2, half)),
            dma((half,)), dma((half,)),
            dma((chunks, half)), dma((chunks, half)),
            dma((chunks, half)), dma((chunks, half)),
            dma((half,)), dma((half,)),
            dma((2,)), dma((2,)),
        ],
        compiler_params=pltpu.CompilerParams(
            collective_id=0, has_side_effects=True, vmem_limit_bytes=60 * 1024 * 1024
        ),
    )(
        context_len,
        exit_depth,
        attn_gain,
        mlp_gain,
        exit_hidden,
        w_query[0],
        w_keyval[0],
        kv_cache.reshape(reqs, ctx * n_kv, 128),
        w_out[0],
        w_gate[0],
        w_up[0],
        w_down[0],
    )
    return out[None]


def solution(mesh):
    in_specs = (
        P("dp", None, ("section", "tensor")),
        P("dp"),
        P("dp"),
        P("section", None),
        P("section", None, "tensor"),
        P("section", None, "tensor"),
        P("section", "tensor", None),
        P("section", "dp", None, "tensor", None),
        P("section", None),
        P("section", "dp", "tensor"),
        P("section", "dp", "tensor"),
        P("section", "dp", "tensor"),
    )
    out_specs = P("section", "dp", None, "tensor")
    count = mesh.shape["dp"]
    fits = (
        mesh.shape["section"] == 2
        and mesh.shape["tensor"] == 2
        and count & (count - 1) == 0
        and count >= 4
        and (D // count) % 128 == 0
    )
    body = fused if fits else local
    return jax.shard_map(body, mesh=mesh, in_specs=in_specs, out_specs=out_specs, check_vma=False)
```

```python
import math

import functools

import jax
import jax.numpy as jnp
from jax import lax
from jax.experimental import pallas as pl
from jax.experimental.pallas import tpu as pltpu
from jax.sharding import PartitionSpec as P

D = 2048
DRAFT = 4
CTX = 384
R_DEV = 8


EPS = 1e-05
THETA = 500000.0
NEGATIVE = -1e30


def shifted(array, axis, by):
    length = lax.axis_size(axis)
    pairs = [(i, i + by) for i in range(length) if 0 <= i + by < length]
    return lax.ppermute(array, axis, pairs)


def rotate(values, where_at):
    middle = values.shape[-1] // 2
    rates = jnp.exp(
        jnp.arange(middle, dtype=jnp.float32) * (-2.0 * math.log(THETA) / values.shape[-1])
    )
    angles = where_at.astype(jnp.float32)[..., None] * rates
    cosine = jnp.cos(angles)
    sine = jnp.sin(angles)
    first = values[..., :middle]
    second = values[..., middle:]
    return jnp.concatenate(
        [first * cosine - second * sine, second * cosine + first * sine], axis=-1
    )


def normalize(hidden, gain):
    wide = hidden.astype(jnp.float32)
    factor = lax.rsqrt(jnp.mean(wide * wide, axis=-1, keepdims=True) + EPS)
    return (wide * factor * gain).astype(jnp.bfloat16)


def attend(normed, lengths, cache, w_query, w_keyval, w_out):
    rows, drafts, width = normed.shape
    head_size = cache.shape[-1] // 2
    kv_count = cache.shape[2]
    q_count = w_query.shape[-1] // head_size
    group = q_count // kv_count
    flat = normed.reshape(rows * drafts, width)
    query = jnp.dot(flat, w_query, preferred_element_type=jnp.float32).reshape(
        rows, drafts, kv_count, group, head_size
    )
    keyval = jnp.dot(flat, w_keyval, preferred_element_type=jnp.float32).reshape(
        rows, drafts, kv_count, 2 * head_size
    )
    places = lengths[:, None] + jnp.arange(drafts, dtype=jnp.int32)[None, :]
    query = rotate(query, places[:, :, None, None]).astype(jnp.bfloat16)
    fresh_keys = rotate(keyval[..., :head_size], places[:, :, None]).astype(jnp.bfloat16)
    fresh_values = keyval[..., head_size:].astype(jnp.bfloat16)
    cached_keys = cache[..., :head_size]
    cached_values = cache[..., head_size:]
    scale = head_size ** (-0.5)
    old_scores = (
        jnp.einsum("rjkgd,rpkd->rkgjp", query, cached_keys, preferred_element_type=jnp.float32)
        * scale
    )
    live = jnp.arange(cache.shape[1], dtype=jnp.int32)[None, :] < lengths[:, None]
    old_scores = jnp.where(live[:, None, None, None, :], old_scores, NEGATIVE)
    new_scores = (
        jnp.einsum("rjkgd,rikd->rkgji", query, fresh_keys, preferred_element_type=jnp.float32)
        * scale
    )
    causal = jnp.arange(drafts)[None, :] <= jnp.arange(drafts)[:, None]
    new_scores = jnp.where(causal, new_scores, NEGATIVE)
    top = jnp.maximum(old_scores.max(axis=-1), new_scores.max(axis=-1))[..., None]
    old_weights = jnp.exp(old_scores - top)
    new_weights = jnp.exp(new_scores - top)
    total = old_weights.sum(axis=-1, keepdims=True) + new_weights.sum(axis=-1, keepdims=True)
    old_weights = (old_weights / total).astype(jnp.bfloat16)
    new_weights = (new_weights / total).astype(jnp.bfloat16)
    mixed = jnp.einsum(
        "rkgjp,rpkd->rjkgd", old_weights, cached_values, preferred_element_type=jnp.float32
    )
    mixed = mixed + jnp.einsum(
        "rkgji,rikd->rjkgd", new_weights, fresh_values, preferred_element_type=jnp.float32
    )
    heads_out = mixed.astype(jnp.bfloat16).reshape(rows * drafts, q_count * head_size)
    return jnp.dot(heads_out, w_out, preferred_element_type=jnp.float32)


def feed_forward(normed, gate_full, up_full, down_full):
    flat = normed.reshape(-1, normed.shape[-1])
    gate = jnp.dot(flat, gate_full, preferred_element_type=jnp.float32)
    up = jnp.dot(flat, up_full, preferred_element_type=jnp.float32)
    act = (jax.nn.silu(gate) * up).astype(jnp.bfloat16)
    return lax.dot_general(
        act, down_full, (((1,), (1,)), ((), ())), preferred_element_type=jnp.float32
    )


def local(
    exit_hidden,
    exit_depth,
    context_len,
    attn_gain,
    w_query,
    w_keyval,
    w_out,
    kv_cache,
    mlp_gain,
    w_gate,
    w_up,
    w_down,
):
    entry = lax.all_gather(exit_hidden, ("section", "tensor"), axis=2, tiled=True)
    gate_full, up_full, down_full = (
        lax.all_gather(w_gate[0], "dp", axis=0, tiled=True),
        lax.all_gather(w_up[0], "dp", axis=0, tiled=True),
        lax.all_gather(w_down[0], "dp", axis=0, tiled=True),
    )
    section = lax.axis_index("section")
    sections = lax.axis_size("section")
    pieces = 1
    members = R_DEV // pieces
    share = D // lax.axis_size("tensor")
    offset = lax.axis_index("tensor") * share
    entry = entry.reshape(pieces, members, DRAFT, D)
    depth = exit_depth.reshape(pieces, members)
    length = context_len.reshape(pieces, members)
    cache = kv_cache[0].reshape(pieces, members, CTX, kv_cache.shape[3], kv_cache.shape[4])
    gain = attn_gain[0]
    second_gain = mlp_gain[0]
    query_weight = w_query[0]
    keyval_weight = w_keyval[0]
    out_weight = w_out[0]

    def turn_step(turn, carry):
        received, outputs = carry
        block = turn - section
        valid = (block >= 0) & (block < pieces)
        index = jnp.clip(block, 0, pieces - 1)
        block_depth = depth[index]
        block_length = length[index]
        block_entry = entry[index]
        block_cache = cache[index]
        take = (block_depth >= section)[:, None, None]
        keep = (block_depth <= section)[:, None, None]
        active = valid & jnp.any(block_depth <= section)

        def compute(whole):
            return attend(
                normalize(whole, gain),
                block_length,
                block_cache,
                query_weight,
                keyval_weight,
                out_weight,
            )

        def branch_work(middle):
            return feed_forward(normalize(middle, second_gain), gate_full, up_full, down_full)

        def skipped(whole):
            return jnp.zeros((members * DRAFT, D), jnp.float32)

        whole = jnp.where(take, block_entry, received)
        partial_value = lax.cond(active, compute, skipped, whole)
        summed = lax.psum(partial_value, "tensor").reshape(members, DRAFT, D)
        middle = (whole.astype(jnp.float32) + summed).astype(jnp.bfloat16)
        branch = lax.cond(active, branch_work, skipped, middle)
        branch_sum = (
            lax.psum(branch.astype(jnp.bfloat16), "tensor")
            .astype(jnp.float32)
            .reshape(members, DRAFT, D)
        )
        updated = (middle.astype(jnp.float32) + branch_sum).astype(jnp.bfloat16)
        result = jnp.where(keep, updated, whole)
        own = lax.dynamic_slice_in_dim(result, offset, share, 2)
        stored = jnp.where(valid, own, outputs[index])
        outputs = lax.dynamic_update_index_in_dim(outputs, stored, index, 0)
        received = shifted(result, "section", 1)
        return (received, outputs)

    carried = D
    start = (
        jnp.zeros((members, DRAFT, carried), jnp.bfloat16),
        jnp.zeros((pieces, members, DRAFT, share), jnp.bfloat16),
    )
    final = lax.fori_loop(0, sections + pieces - 1, turn_step, start)
    return final[1]


MESH = pl.DeviceIdType.MESH
CHUNKS = 4
BF = jnp.bfloat16
F32 = jnp.float32


def bits(size):
    return size.bit_length() - 1


def mm(a, b):
    return jnp.dot(a, b, preferred_element_type=F32)


def mm_t(a, b):
    return lax.dot_general(a, b, (((1,), (1,)), ((), ())), preferred_element_type=F32)


def lanes_like(shape):
    return lax.broadcasted_iota(jnp.int32, shape, len(shape) - 1)


def fused_kernel(
    ndp,
    lens_ref,
    depth_ref,
    gain_ref,
    gain2_ref,
    entry_ref,
    wq_hbm,
    wkv_hbm,
    kv_hbm,
    wo_hbm,
    wg_hbm,
    wu_hbm,
    wd_hbm,
    out_ref,
    wq, wkv, kv, wo, wg, wu, wd,
    ent, ew, cur, perms, whb, qs, kvs, qp, ns, oh, heads,
    p1, mids, mid, xs, sqs, sqr,
    zbuf, zrec, acts, fbuf, fin, res,
    ld_sem, w_s, w_r, go, ent_s, ent_r, a_s, a_r, q_s, q_r, z_s, z_r,
    g_s, g_r, f_s, f_r, c_s, c_r,
):
    s = lax.axis_index("section")
    t = lax.axis_index("tensor")
    d = lax.axis_index("dp")
    half = ndp // 2
    z = d // 2
    y = d % 2
    twin = d + 1 - 2 * y
    reqs, drafts, piece = entry_ref.shape
    tok = reqs * drafts
    width = gain_ref.shape[1]
    fb = width // half
    n_heads = wq.shape[1] // 64
    n_kv = wkv.shape[1] // 128
    ff = wg.shape[2]
    chunks, cw = acts.shape[0], acts.shape[3]
    rows = n_heads * drafts

    loads = [
        pltpu.make_async_copy(src, dst, ld_sem.at[i])
        for i, (src, dst) in enumerate(
            [
                (wq_hbm, wq),
                (wkv_hbm, wkv),
                (kv_hbm, kv),
                (wo_hbm, wo),
                (wg_hbm, wg.at[y]),
                (wu_hbm, wu.at[y]),
                (wd_hbm, wd.at[y]),
            ]
        )
    ]
    for one in loads:
        one.start()

    barrier = pltpu.get_barrier_semaphore()
    lane_me = t * half + z
    for k in range(1, 2 * half):
        peer = (lane_me + k) % (2 * half)
        where = (s, peer // half, peer % half * 2 + y)
        pl.semaphore_signal(barrier, inc=1, device_id=where, device_id_type=MESH)
    for k in range(2):
        pl.semaphore_signal(barrier, inc=1, device_id=(1 - s, k, d), device_id_type=MESH)
    pl.semaphore_signal(barrier, inc=1, device_id=(s, t, twin), device_id_type=MESH)
    pl.semaphore_wait(barrier, 2 * half + 2)

    def remote(src, dst, send, recv, where):
        return pltpu.make_async_remote_copy(
            src_ref=src, dst_ref=dst, send_sem=send, recv_sem=recv, device_id=where, device_id_type=MESH
        )

    def twin_copy(k):
        if k == 2 * chunks:
            return remote(wd_hbm, wd.at[y], w_s.at[k], w_r.at[k], (s, t, twin))
        src, dst = [(wg_hbm, wg), (wu_hbm, wu)][k % 2]
        cols = pl.ds(k // 2 * cw, cw)
        return remote(src.at[:, cols], dst.at[y, :, cols], w_s.at[k], w_r.at[k], (s, t, twin))

    mine = s * 2 + t
    pending = []
    for k in range(1, 4):
        other = (mine + k) % 4
        copy = remote(entry_ref, ent.at[mine], ent_s.at[k - 1], ent_r.at[mine], (other // 2, other % 2, d))
        copy.start()
        pending.append(copy)
    ent[mine] = entry_ref[...]

    @pl.when(s == 0)
    def _():
        for k in range(2 * chunks + 1):
            twin_copy(k).start()

    def permutation(transposed):
        i = lax.broadcasted_iota(jnp.int32, (n_heads * tok,) * 2, 1 if transposed else 0)
        c = lax.broadcasted_iota(jnp.int32, (n_heads * tok,) * 2, 0 if transposed else 1)
        bd, bt, br = bits(drafts), bits(tok), bits(rows)
        target = ((i & (rows - 1)) >> bd << bt) + (i >> br << bd) + (i & (drafts - 1))
        return jnp.where(target == c, 1.0, 0.0).astype(BF)

    perms[0] = permutation(False)
    perms[1] = permutation(True)
    row = lax.broadcasted_iota(jnp.int32, (tok, 128), 0)
    lane = lanes_like((tok, 128))
    low = (lane & 63) < 32
    left = lane < 64
    length = jnp.zeros((tok, 128), jnp.int32)
    depth = jnp.zeros((tok, 128), jnp.int32)
    for r in range(reqs):
        here = (row >> bits(drafts)) == r
        length = jnp.where(here, lens_ref[r], length)
        depth = jnp.where(here, depth_ref[r], depth)
    rates = jnp.exp((lane & 31).astype(F32) * (-2.0 * math.log(THETA) / 64))
    angles = (length + (row & (drafts - 1))).astype(F32) * rates
    cosine = jnp.cos(angles)
    sine = jnp.where(low, -1.0, 1.0) * jnp.sin(angles)
    take = depth[:, :1] >= s
    keep = depth[:, :1] <= s

    for k in range(1, 4):
        other = (mine + k) % 4
        remote(entry_ref, ent.at[other], ent_s.at[k - 1], ent_r.at[other], (other // 2, other % 2, d)).wait_recv()

    for q in range(4):
        for r in range(reqs):
            ew[r * drafts : (r + 1) * drafts, q * piece : (q + 1) * piece] = ent[q, r].astype(F32)

    @pl.when(s == 0)
    def _():
        cur[...] = jnp.zeros_like(cur)

    @pl.when(s == 1)
    def _():
        pl.semaphore_wait(go, 1)
        for k in range(2 * chunks + 1):
            twin_copy(k).start()
        for k in range(2):
            remote(res, cur.at[k], c_s.at[k], c_r.at[k], (0, k, d)).wait_recv()

    wide = []
    total_sq = None
    per_cur = cur.shape[2] // fb
    for b in range(half):
        e = ew[:, b * fb : (b + 1) * fb]
        c = cur[b // per_cur, :, (b % per_cur) * fb : (b % per_cur + 1) * fb].astype(F32)
        w = jnp.where(take, e, c)
        whb[b] = w.astype(BF)
        wide.append(w)
        sq = jnp.sum(w * w, axis=-1, keepdims=True)
        total_sq = sq if total_sq is None else total_sq + sq
    factor = lax.rsqrt(total_sq * (1.0 / width) + EPS)
    normed = jnp.concatenate(
        [(w * factor * gain_ref[:, b * fb : (b + 1) * fb]).astype(BF) for b, w in enumerate(wide)], axis=1
    )

    loads[0].wait()
    for i in range(wq.shape[1] // 256):
        qs[:, i * 256 : (i + 1) * 256] = mm(normed, wq[:, i * 256 : (i + 1) * 256])
    loads[1].wait()
    for i in range(wkv.shape[1] // 256):
        kvs[:, i * 256 : (i + 1) * 256] = mm(normed, wkv[:, i * 256 : (i + 1) * 256])

    def turned(x):
        partner = jnp.where(low, pltpu.roll(x, 96, 1), pltpu.roll(x, 32, 1))
        return x * cosine + partner * sine

    stacked = []
    for b in range(n_heads // 2):
        x = turned(qs[:, b * 128 : (b + 1) * 128]) * (64 ** -0.5)
        stacked.append(jnp.where(left, x, 0.0).astype(BF))
        stacked.append(jnp.where(left, pltpu.roll(x, 64, 1), 0.0).astype(BF))
    qp[...] = mm(perms[0], jnp.concatenate(stacked, axis=0)).astype(BF)
    fresh = []
    for h in range(n_kv):
        x = kvs[:, h * 128 : (h + 1) * 128]
        fresh.append(jnp.where(left, turned(x), x).astype(BF))
    fresh = jnp.concatenate(fresh, axis=0)

    ri = lax.broadcasted_iota(jnp.int32, (reqs * rows, n_kv * tok), 0)
    ci = lax.broadcasted_iota(jnp.int32, (reqs * rows, n_kv * tok), 1)
    bg = bits(rows // n_kv)
    allowed = (
        ((ri >> bits(rows)) == ((ci & (tok - 1)) >> bits(drafts)))
        & (((ri & (rows - 1)) >> bg) == (ci >> bits(tok)))
        & ((ci & (drafts - 1)) <= (ri & (drafts - 1)))
    )
    ns[...] = jnp.where(allowed, mm_t(qp[...], fresh), NEGATIVE)

    loads[2].wait()
    ctx = kv.shape[1] // n_kv
    slot = lax.broadcasted_iota(jnp.int32, (rows, ctx * n_kv), 1)
    group = lax.broadcasted_iota(jnp.int32, (rows, ctx * n_kv), 0) >> bg
    same = (slot & (n_kv - 1)) == group
    for r in range(reqs):
        cached = kv[r]
        old = mm_t(qp[r * rows : (r + 1) * rows], cached)
        old = jnp.where(same & (slot < n_kv * lens_ref[r]), old, NEGATIVE)
        new = ns[r * rows : (r + 1) * rows]
        top = jnp.maximum(jnp.max(old, axis=1, keepdims=True), jnp.max(new, axis=1, keepdims=True))
        old = jnp.exp(old - top)
        new = jnp.exp(new - top)
        total = jnp.sum(old, axis=1, keepdims=True) + jnp.sum(new, axis=1, keepdims=True)
        mixed = mm(old.astype(BF), cached) + mm(new.astype(BF), fresh)
        oh[r * rows : (r + 1) * rows] = (mixed / total).astype(BF)

    back = mm(perms[1], oh[...])
    for b in range(n_heads // 2):
        first = back[2 * b * tok : (2 * b + 1) * tok]
        second = back[(2 * b + 1) * tok : (2 * b + 2) * tok]
        heads[:, b * 128 : (b + 1) * 128] = jnp.where(left, pltpu.roll(first, 64, 1), second).astype(BF)

    loads[3].wait()

    def project(i):
        b = (z + 1 + i) % half
        part = mm(heads[...], wo[:, pl.ds(pl.multiple_of(b * fb, fb), fb)])
        p1[b] = (part + 0.5 * whb[b].astype(F32)).astype(BF)
        return b

    def to_all(i, k):
        b = project(i)
        for u in range(2):
            remote(p1.at[b], mids.at[t, z], a_s.at[u, b], a_r.at[t, z], (s, u, b * 2 + y)).start()
        return k

    lax.fori_loop(0, half - 1, to_all, 0)
    project(half - 1)
    remote(p1.at[z], mids.at[t, z], a_s.at[1 - t, z], a_r.at[t, z], (s, 1 - t, d)).start()
    mids[t, z] = p1[z]

    others = []
    for k in range(1, 2 * half):
        peer = (lane_me + k) % (2 * half)
        others.append((peer // half, peer % half))
    for pt, pz in others:
        remote(p1.at[pz], mids.at[pt, pz], a_s.at[pt, pz], a_r.at[pt, pz], (s, pt, pz * 2 + y)).wait_recv()

    gain2 = gain2_ref[:, pl.ds(pl.multiple_of(z * fb, fb), fb)]
    for b in range(half):
        m = (mids[0, b].astype(F32) + mids[1, b].astype(F32)).astype(BF)
        mid[b] = m
        m = m.astype(F32)
        sq = m * m
        part = sq[:, :128]
        for j in range(1, fb // 128):
            part = part + sq[:, j * 128 : (j + 1) * 128]
        sqs[b] = part
        xs[b] = (m * gain2).astype(BF)
    order = [(z + k) % half for k in range(1, half)]
    for zz in order:
        remote(sqs.at[zz], sqr.at[z], q_s.at[zz], q_r.at[z], (s, t, zz * 2 + y)).start()
    sqr[z] = sqs[z]

    loads[4].wait()
    loads[5].wait()
    grid = xs[...].reshape(half * tok, fb)
    step = 512
    for c in range(chunks):
        twin_copy(2 * c).wait()
        twin_copy(2 * c + 1).wait()
        for i in range(cw // step):
            src = slice(c * cw + i * step, c * cw + (i + 1) * step)
            for g, w in enumerate((wg, wu)):
                dst = slice(g * cw + i * step, g * cw + (i + 1) * step)
                zbuf[c, :, :, dst] = mm(grid, w[:, :, src].reshape(fb, step)).astype(BF).reshape(half, tok, step)
        for zz in order:
            remote(zbuf.at[c, zz], zrec.at[c, z], z_s.at[c, zz], z_r.at[c, z], (s, t, zz * 2 + y)).start()

    for zz in order:
        remote(sqs.at[zz], sqr.at[zz], q_s.at[zz], q_r.at[zz], (s, t, zz * 2 + y)).wait_recv()
    sums = sqr[0]
    for b in range(1, half):
        sums = sums + sqr[b]
    scale = lax.rsqrt(jnp.sum(sums, axis=1, keepdims=True) * (1.0 / width) + EPS)
    for c in range(chunks):
        if c == chunks - 1:
            twin_copy(2 * chunks).wait()

            @pl.when(s == 0)
            def _():
                pl.semaphore_signal(go, inc=1, device_id=(1, t, d), device_id_type=MESH)

        for zz in order:
            remote(zbuf.at[c, zz], zrec.at[c, zz], z_s.at[c, zz], z_r.at[c, zz], (s, t, zz * 2 + y)).wait_recv()
        for i in range(cw // step):
            pair = []
            for start in (i * step, cw + i * step):
                cols = slice(start, start + step)
                v = zbuf[c, z, :, cols].astype(F32)
                for zz in order:
                    v = v + zrec[c, zz, :, cols].astype(F32)
                pair.append(v * scale)
            gate, up = pair
            acts[c, z, :, i * step : (i + 1) * step] = (gate / (1.0 + jnp.exp(-gate)) * up).astype(BF)
        for zz in order:
            remote(acts.at[c, z], acts.at[c, z], g_s.at[c, zz], g_r.at[c, z], (s, t, zz * 2 + y)).start()

    loads[6].wait()
    grown = None
    for c in range(chunks):
        for zz in order:
            remote(acts.at[c, zz], acts.at[c, zz], g_s.at[c, zz], g_r.at[c, zz], (s, t, zz * 2 + y)).wait_recv()
        part = mm_t(acts[c].reshape(half * tok, cw), wd[:, :, c * cw : (c + 1) * cw].reshape(fb, cw))
        grown = part if grown is None else grown + part

    per_home = half // 2
    home = z // per_home
    place = t * per_home + z % per_home
    for b in range(half):
        fbuf[b] = (grown[b * tok : (b + 1) * tok] + 0.5 * mid[b].astype(F32)).astype(BF)
    for zz in order:
        remote(fbuf.at[zz], fin.at[place], f_s.at[zz], f_r.at[place], (s, home, zz * 2 + y)).start()

    @pl.when(home != t)
    def _():
        remote(fbuf.at[z], fin.at[place], f_s.at[z], f_r.at[place], (s, home, d)).start()

    @pl.when(home == t)
    def _():
        fin[place] = fbuf[z]

    for k in range(half):
        src_t, src_z = k // per_home, t * per_home + k % per_home

        @pl.when(jnp.logical_not((src_t == t) & (src_z == z)))
        def _():
            remote(fbuf.at[0], fin.at[k], f_s.at[0], f_r.at[k], (s, src_t, src_z * 2 + y)).wait_recv()

    for j in range(per_home):
        updated = (fin[j].astype(F32) + fin[per_home + j].astype(F32)).astype(BF).astype(F32)
        value = jnp.where(keep, updated, whb[t * per_home + j].astype(F32))
        res[:, j * fb : (j + 1) * fb] = value.astype(BF)
        ew[:, j * fb : (j + 1) * fb] = value

    @pl.when(s == 0)
    def _():
        for k in range(2):
            remote(res, cur.at[t], c_s.at[k], c_r.at[t], (1, k, d)).start()

    for r in range(reqs):
        out_ref[r] = ew[r * drafts : (r + 1) * drafts, : width // 2].astype(BF)

    @pl.when(s == 0)
    def _():
        for k in range(2):
            remote(res, cur.at[t], c_s.at[k], c_r.at[t], (1, k, d)).wait_send()

    for copy in pending:
        copy.wait_send()
    for pt, pz in others:
        remote(p1.at[pz], mids.at[t, z], a_s.at[pt, pz], a_r.at[pt, pz], (s, pt, pz * 2 + y)).wait_send()
    for zz in order:
        remote(sqs.at[zz], sqr.at[z], q_s.at[zz], q_r.at[z], (s, t, zz * 2 + y)).wait_send()
        for c in range(chunks):
            remote(zbuf.at[c, zz], zrec.at[c, z], z_s.at[c, zz], z_r.at[c, z], (s, t, zz * 2 + y)).wait_send()
            remote(acts.at[c, z], acts.at[c, z], g_s.at[c, zz], g_r.at[c, z], (s, t, zz * 2 + y)).wait_send()
        remote(fbuf.at[zz], fin.at[place], f_s.at[zz], f_r.at[place], (s, home, zz * 2 + y)).wait_send()

    @pl.when(home != t)
    def _():
        remote(fbuf.at[z], fin.at[place], f_s.at[z], f_r.at[place], (s, home, d)).wait_send()


def fused(
    exit_hidden,
    exit_depth,
    context_len,
    attn_gain,
    w_query,
    w_keyval,
    w_out,
    kv_cache,
    mlp_gain,
    w_gate,
    w_up,
    w_down,
):
    ndp = lax.axis_size("dp")
    reqs, drafts, piece = exit_hidden.shape
    tok = reqs * drafts
    width = w_query.shape[1]
    half = ndp // 2
    fb = width // half
    ff = w_gate.shape[2]
    n_kv = kv_cache.shape[3]
    ctx = kv_cache.shape[2]
    q_cols = w_query.shape[2]
    n_heads = q_cols // 64
    chunks = CHUNKS
    cw = ff // chunks
    hbm = pl.BlockSpec(memory_space=pl.ANY)
    vmem = pl.BlockSpec(memory_space=pltpu.VMEM)
    smem = pl.BlockSpec(memory_space=pltpu.SMEM)
    dma = pltpu.SemaphoreType.DMA
    V = pltpu.VMEM
    out = pl.pallas_call(
        functools.partial(fused_kernel, ndp),
        out_shape=jax.ShapeDtypeStruct((reqs, drafts, width // 2), BF),
        in_specs=[smem, smem, vmem, vmem, vmem] + [hbm] * 7,
        out_specs=vmem,
        scratch_shapes=[
            V(w_query.shape[1:], BF),
            V(w_keyval.shape[1:], BF),
            V((reqs, ctx * n_kv, 128), BF),
            V(w_out.shape[1:], BF),
            V((2, fb // 2, ff), BF),
            V((2, fb // 2, ff), BF),
            V((2, fb // 2, ff), BF),
            V((4, reqs, drafts, piece), BF),
            V((tok, width), F32),
            V((2, tok, width // 2), BF),
            V((2, n_heads * tok, n_heads * tok), BF),
            V((half, tok, fb), BF),
            V((tok, q_cols), F32),
            V((tok, n_kv * 128), F32),
            V((n_heads * tok, 128), BF),
            V((n_heads * tok, n_kv * tok), F32),
            V((n_heads * tok, 128), BF),
            V((tok, q_cols), BF),
            V((half, tok, fb), BF),
            V((2, half, tok, fb), BF),
            V((half, tok, fb), BF),
            V((half, tok, fb), BF),
            V((half, tok, 128), F32),
            V((half, tok, 128), F32),
            V((chunks, half, tok, 2 * cw), BF),
            V((chunks, half, tok, 2 * cw), BF),
            V((chunks, half, tok, cw), BF),
            V((half, tok, fb), BF),
            V((half, tok, fb), BF),
            V((tok, width // 2), BF),
            dma((7,)),
            dma((2 * chunks + 1,)), dma((2 * chunks + 1,)), pltpu.SemaphoreType.REGULAR,
            dma((3,)), dma((4,)),
            dma((2, half)), dma((2, half)),
            dma((half,)), dma((half,)),
            dma((chunks, half)), dma((chunks, half)),
            dma((chunks, half)), dma((chunks, half)),
            dma((half,)), dma((half,)),
            dma((2,)), dma((2,)),
        ],
        compiler_params=pltpu.CompilerParams(
            collective_id=0, has_side_effects=True, vmem_limit_bytes=60 * 1024 * 1024
        ),
    )(
        context_len,
        exit_depth,
        attn_gain,
        mlp_gain,
        exit_hidden,
        w_query[0],
        w_keyval[0],
        kv_cache.reshape(reqs, ctx * n_kv, 128),
        w_out[0],
        w_gate[0],
        w_up[0],
        w_down[0],
    )
    return out[None]


def solution(mesh):
    in_specs = (
        P("dp", None, ("section", "tensor")),
        P("dp"),
        P("dp"),
        P("section", None),
        P("section", None, "tensor"),
        P("section", None, "tensor"),
        P("section", "tensor", None),
        P("section", "dp", None, "tensor", None),
        P("section", None),
        P("section", "dp", "tensor"),
        P("section", "dp", "tensor"),
        P("section", "dp", "tensor"),
    )
    out_specs = P("section", "dp", None, "tensor")
    count = mesh.shape["dp"]
    fits = (
        mesh.shape["section"] == 2
        and mesh.shape["tensor"] == 2
        and count & (count - 1) == 0
        and count >= 4
        and (D // count) % 128 == 0
    )
    body = fused if fits else local
    return jax.shard_map(body, mesh=mesh, in_specs=in_specs, out_specs=out_specs, check_vma=False)
```
